1024 devices in a mesh: row: 32 (over x, y_lo), col: 32 (over y_hi, z, core).
Axes of the slice: x: 8, y: 8 (y_hi: 2, y_lo: 4; y = y_hi * 4 + y_lo), z: 8, core: 2. Of those that a mesh axis runs over, the one named last changes fastest.
Arguments:
- embeddings: bfloat16 [512, 256, 256], P('col'), may hold values from -0.375 to 0.375
- projection: bfloat16 [256, 64], replicated, may hold values from -4.1875 to 4.1875
- weight: bfloat16 [16384, 32768], P('row', 'col'), may hold values from -0.046875 to 0.046875
- act_grad: bfloat16 [512, 32768], P('row', 'col'), may hold values from -6 to 6
Outputs:
- activation: bfloat16 [512, 32768], P('row', 'col')
- weight_grad: float32 [16384, 32768], P('row', 'col')
- feature_grad: float32 [512, 16384], P('col', 'row')
The draws below stay inside these ranges and needn't reach their ends.
All inputs are finite; a program needn't handle non-finite values.
Results may differ from the reference program's by a relative error of at most 0.0066.
Values may be sent and summed in bfloat16 or wider, within the bound.
No kernel may reach another device: no remote copies, remote signals or barrier semaphores. Data moves between devices by JAX's collectives and lax.ppermute only.
A program may use at most 32 MiB of HBM per device.

```python
import jax
import jax.numpy as jnp
from jax import lax

N_EMB = 256
D_EMB = 256
PROJ = 64
H = 32768
B = 512
K = 16384


def level_of(key, shape, cuts, low, high):
    def one(dim, parts):
        heights = jax.random.uniform(jax.random.fold_in(jax.random.fold_in(key, 6), dim), (parts,), jnp.float32, low / len(cuts), high / len(cuts))
        return jnp.repeat(jnp.exp(heights), shape[dim] // parts).reshape((-1,) + (1,) * (len(shape) - dim - 1))

    factor_of = one(*cuts[0])
    for cut in cuts[1:]:
        factor_of = factor_of * one(*cut)
    return factor_of


def noise(stream_key, dims, width, bound, shards=(), kind=jnp.bfloat16):
    drawn = jax.random.normal(stream_key, dims, jnp.float32) * width
    if len(shards) > 0:
        drawn = level_of(stream_key, dims, shards, -0.22, 0.18) * drawn
    return jnp.clip(drawn, min=-bound, max=bound).astype(kind)


def setup_inputs(seed: int = 0) -> dict:
    seeds = jax.random.split(jax.random.key(seed), 5)
    return {
        "embeddings": noise(seeds[0], (B, N_EMB, D_EMB), D_EMB ** -0.5, 0.375, ((0, 32),)),
        "projection": noise(seeds[1], (N_EMB, PROJ), 0.7, 4.1875),
        "weight": noise(seeds[2], (K, H), K ** -0.5, 0.046875, ((0, 32), (1, 32))),
        "act_grad": noise(seeds[3], (B, H), 1.0, 6.0, ((0, 32), (1, 32))),
    }


def silu_slope(values):
    sig = jax.nn.sigmoid(values)
    return sig * (1.0 + values * (1.0 - sig))


def reference(embeddings, projection, weight, act_grad):
    emb_wide = embeddings.astype(jnp.float32)
    gram = jnp.einsum('bid,bmd->bim', emb_wide, emb_wide).astype(jnp.bfloat16)
    features = jnp.einsum('bim,mr->bir', gram.astype(jnp.float32), projection.astype(jnp.float32))
    features = features.astype(jnp.bfloat16).reshape(embeddings.shape[0], -1)
    preact = jnp.dot(features, weight, preferred_element_type=jnp.float32)
    activation = jax.nn.silu(preact).astype(jnp.bfloat16)
    slope_grad = (act_grad.astype(jnp.float32) * silu_slope(preact)).astype(jnp.bfloat16)
    weight_grad = lax.dot_general(features, slope_grad, (((0,), (0,)), ((), ())), preferred_element_type=jnp.float32)
    feature_grad = lax.dot_general(slope_grad, weight, (((1,), (1,)), ((), ())), preferred_element_type=jnp.float32)
    return activation, weight_grad, feature_grad
```

```python
import jax
import jax.numpy as jnp
from jax import lax
from jax.sharding import PartitionSpec as P

BF16 = jnp.bfloat16
F32 = jnp.float32


def silu_slope(values):
    sig = jax.nn.sigmoid(values)
    return sig * (1.0 + values * (1.0 - sig))


def gather_rows(part, axis, size):
    copies = jnp.broadcast_to(part[None], (size, *part.shape))
    got = lax.all_to_all(copies, axis, 0, 0)
    return got.reshape(size * part.shape[0], *part.shape[1:])


def sum_scatter_rows(total, axis, size):
    shares = total.astype(BF16).reshape(size, total.shape[0] // size, *total.shape[1:])
    got = lax.all_to_all(shares, axis, 0, 0)
    return jnp.sum(got.astype(F32), axis=0)


def make_shards(rows, cols):
    def shards(embeddings, projection, weight, act_grad):
        emb_rows = weight.shape[0] // projection.shape[1]
        emb_first = lax.axis_index("row") * emb_rows
        mine_emb = lax.dynamic_slice_in_dim(embeddings, emb_first, emb_rows, 1)
        interaction = jnp.einsum(
            "bid,bmd->bim", mine_emb, embeddings, preferred_element_type=F32
        ).astype(BF16)
        local_features = jnp.einsum(
            "bim,mr->bir", interaction, projection, preferred_element_type=F32
        )
        local_features = local_features.astype(BF16).reshape(embeddings.shape[0], -1)
        features_all = gather_rows(local_features, "col", cols)
        preact = sum_scatter_rows(
            jnp.dot(features_all, weight, preferred_element_type=F32), "row", rows
        )
        activation = jax.nn.silu(preact).astype(BF16)
        slope_mine = (act_grad.astype(F32) * silu_slope(preact)).astype(BF16)
        slope_all = gather_rows(slope_mine, "row", rows)
        feature_grad = sum_scatter_rows(
            lax.dot_general(
                slope_all, weight, (((1,), (1,)), ((), ())), preferred_element_type=F32
            ),
            "col",
            cols,
        )
        weight_grad = lax.dot_general(
            features_all, slope_all, (((0,), (0,)), ((), ())), preferred_element_type=F32
        )
        return (activation, weight_grad, feature_grad)

    return shards


def solution(mesh):
    return jax.shard_map(
        make_shards(mesh.shape["row"], mesh.shape["col"]),
        mesh=mesh,
        in_specs=(P("col", None, None), P(), P("row", "col"), P("row", "col")),
        out_specs=(P("row", "col"), P("row", "col"), P("col", "row")),
        check_vma=False,
    )
```

```python
import jax
import jax.numpy as jnp
from jax import lax
from jax.sharding import PartitionSpec as P

BF16 = jnp.bfloat16
F32 = jnp.float32


def silu_slope(values):
    sig = jax.nn.sigmoid(values)
    return sig * (1.0 + values * (1.0 - sig))


def send_copies(part, axis, groups):
    copies = jnp.broadcast_to(part[None], (len(groups[0]), *part.shape))
    return lax.all_to_all(copies, axis, 0, 0, axis_index_groups=groups)


def send_shares(shares, axis, groups):
    got = lax.all_to_all(shares, axis, 0, 0, axis_index_groups=groups)
    return jnp.sum(got.astype(F32), axis=0)


def make_shards(rows, cols):
    pairs = [[c, c + 1] for c in range(0, cols, 2)]
    cores = [list(range(core, cols, 2)) for core in range(2)]
    row_order = [[*range(0, rows, 2), *range(1, rows, 2)]]
    swap = [(c, c ^ 1) for c in range(cols)]

    def shards(embeddings, projection, weight, act_grad):
        mine_b = embeddings.shape[0]
        emb_rows = weight.shape[0] // projection.shape[1]
        emb_first = lax.axis_index("row") * emb_rows
        core = lax.axis_index("col") % 2
        mine_emb = lax.dynamic_slice_in_dim(embeddings, emb_first, emb_rows, 1)
        interaction = jnp.einsum(
            "bid,bmd->bim", mine_emb, embeddings, preferred_element_type=F32
        ).astype(BF16)
        local_features = jnp.einsum(
            "bim,mr->bir", interaction, projection, preferred_element_type=F32
        )
        local_features = local_features.astype(BF16).reshape(mine_b, -1)
        same_core = send_copies(local_features, "col", cores)
        same_core = same_core.reshape(-1, same_core.shape[-1])
        features_all = lax.all_gather(
            same_core, "col", axis=0, axis_index_groups=pairs, tiled=True
        )
        partial = jnp.dot(features_all, weight, preferred_element_type=F32).astype(BF16)
        preact = send_shares(
            partial.reshape(rows, -1, partial.shape[-1]), "row", row_order
        )
        slope_mine = (act_grad.astype(F32) * silu_slope(preact)).astype(BF16)
        activation = jax.nn.silu(preact).astype(BF16)
        slope_all = send_copies(slope_mine, "row", row_order)
        slope_all = slope_all.reshape(-1, slope_all.shape[-1])
        half = slope_all.shape[0] // 2

        def grad_of(which):
            mine = lax.dynamic_slice_in_dim(slope_all, which * half, half, 0)
            return lax.dot_general(
                mine, weight, (((1,), (1,)), ((), ())), preferred_element_type=F32
            )

        got = lax.ppermute(grad_of(1 - core).astype(BF16), "col", swap)
        chip_sum = (grad_of(core) + got.astype(F32)).astype(BF16)
        feature_grad = send_shares(
            chip_sum.reshape(cols // 2, mine_b, -1), "col", cores
        )
        weight_grad = lax.dot_general(
            features_all, slope_all, (((0,), (0,)), ((), ())), preferred_element_type=F32
        )
        return (activation, weight_grad, feature_grad)

    return shards


def solution(mesh):
    return jax.shard_map(
        make_shards(mesh.shape["row"], mesh.shape["col"]),
        mesh=mesh,
        in_specs=(P("col", None, None), P(), P("row", "col"), P("row", "col")),
        out_specs=(P("row", "col"), P("row", "col"), P("col", "row")),
        check_vma=False,
    )
```

```python
import jax
import jax.numpy as jnp
from jax import lax
from jax.sharding import PartitionSpec as P

BF16 = jnp.bfloat16
F32 = jnp.float32


def silu_slope(values):
    sig = jax.nn.sigmoid(values)
    return sig * (1.0 + values * (1.0 - sig))


def send_copies(part, axis, groups):
    copies = jnp.broadcast_to(part[None], (len(groups[0]), *part.shape))
    return lax.all_to_all(copies, axis, 0, 0, axis_index_groups=groups)


def send_shares(shares, axis, groups):
    got = lax.all_to_all(shares, axis, 0, 0, axis_index_groups=groups)
    return jnp.sum(got.astype(F32), axis=0)


def make_shards(rows, cols):
    pairs = [[c, c + 1] for c in range(0, cols, 2)]
    cores = [list(range(core, cols, 2)) for core in range(2)]
    row_order = [[*range(0, rows, 2), *range(1, rows, 2)]]

    def shards(embeddings, projection, weight, act_grad):
        mine_b = embeddings.shape[0]
        emb_rows = weight.shape[0] // projection.shape[1]
        emb_first = lax.axis_index("row") * emb_rows
        mine_emb = lax.dynamic_slice_in_dim(embeddings, emb_first, emb_rows, 1)
        interaction = jnp.einsum(
            "bid,bmd->bim", mine_emb, embeddings, preferred_element_type=F32
        ).astype(BF16)
        local_features = jnp.einsum(
            "bim,mr->bir", interaction, projection, preferred_element_type=F32
        )
        local_features = local_features.astype(BF16).reshape(mine_b, -1)
        same_core = send_copies(local_features, "col", cores)
        same_core = same_core.reshape(-1, same_core.shape[-1])
        features_all = lax.all_gather(
            same_core, "col", axis=0, axis_index_groups=pairs, tiled=True
        )
        partial = jnp.dot(features_all, weight, preferred_element_type=F32).astype(BF16)
        preact = send_shares(
            partial.reshape(rows, -1, partial.shape[-1]), "row", row_order
        )
        slope_mine = (act_grad.astype(F32) * silu_slope(preact)).astype(BF16)
        activation = jax.nn.silu(preact).astype(BF16)
        slope_all = send_copies(slope_mine, "row", row_order)
        slope_all = slope_all.reshape(-1, slope_all.shape[-1])
        partial_grad = lax.dot_general(
            slope_all, weight, (((1,), (1,)), ((), ())), preferred_element_type=F32
        ).astype(BF16)
        chip_sum = send_shares(
            partial_grad.reshape(2, -1, partial_grad.shape[-1]), "col", pairs
        ).astype(BF16)
        feature_grad = send_shares(
            chip_sum.reshape(cols // 2, mine_b, -1), "col", cores
        )
        weight_grad = lax.dot_general(
            features_all, slope_all, (((0,), (0,)), ((), ())), preferred_element_type=F32
        )
        return (activation, weight_grad, feature_grad)

    return shards


def solution(mesh):
    return jax.shard_map(
        make_shards(mesh.shape["row"], mesh.shape["col"]),
        mesh=mesh,
        in_specs=(P("col", None, None), P(), P("row", "col"), P("row", "col")),
        out_specs=(P("row", "col"), P("row", "col"), P("col", "row")),
        check_vma=False,
    )
```

```python
import jax
import jax.numpy as jnp
from jax import lax
from jax.sharding import PartitionSpec as P

BF16 = jnp.bfloat16
F32 = jnp.float32


def silu_slope(values):
    sig = jax.nn.sigmoid(values)
    return sig * (1.0 + values * (1.0 - sig))


def send_copies(part, axis, groups=None):
    size = len(groups[0]) if groups else lax.axis_size(axis)
    copies = jnp.broadcast_to(part[None], (size, *part.shape))
    got = lax.all_to_all(copies, axis, 0, 0, axis_index_groups=groups)
    return got.reshape(-1, got.shape[-1])


def send_shares(shares, axis, groups=None):
    got = lax.all_to_all(shares, axis, 0, 0, axis_index_groups=groups)
    return jnp.sum(got.astype(F32), axis=0)


def either(flag, first, second, axis):
    return jnp.where(
        flag,
        jnp.concatenate([first, second], axis),
        jnp.concatenate([second, first], axis),
    )


def make_shards(rows, cols):
    cores = [list(range(core, cols, 2)) for core in range(2)]
    swap = [(c, c ^ 1) for c in range(cols)]
    spread, spread_far = [], []
    for row in range(rows):
        for col in range(cols):
            h, k = row % 2, col % 2
            spread.append((row * cols + col, (row - h + k) * cols + col - k + h))
            spread_far.append((row * cols + col, (row - h + 1 - k) * cols + col - k + h))
    collect = [(b, a) for a, b in spread]
    collect_far = [(b, a) for a, b in spread_far]

    def shards(embeddings, projection, weight, act_grad):
        mine_b, width = act_grad.shape
        half = mine_b // 2
        emb_rows = weight.shape[0] // projection.shape[1]
        emb_first = lax.axis_index("row") * emb_rows
        h, k = lax.axis_index("row") % 2, lax.axis_index("col") % 2

        mine_emb = lax.dynamic_slice_in_dim(embeddings, emb_first, emb_rows, 1)
        interaction = jnp.einsum(
            "bid,bmd->bim", mine_emb, embeddings, preferred_element_type=F32
        ).astype(BF16)
        local_features = jnp.einsum(
            "bim,mr->bir", interaction, projection, preferred_element_type=F32
        )
        local_features = local_features.astype(BF16).reshape(mine_b, -1)
        local_features, weight_late = lax.optimization_barrier((local_features, weight))
        features = send_copies(local_features, "col", cores)

        both_weights = jnp.concatenate(
            [weight, lax.ppermute(weight_late, "col", swap)], 1
        )
        halves = act_grad.reshape(2, half, width)
        near = lax.ppermute(
            lax.dynamic_index_in_dim(halves, k, 0, False), ("row", "col"), spread
        )
        far = lax.ppermute(
            lax.dynamic_index_in_dim(halves, 1 - k, 0, False), ("row", "col"), spread_far
        )
        both_grads = either(h == k, near, far, 1).astype(F32)

        partial = jnp.dot(features, both_weights, preferred_element_type=F32)
        preact = send_shares(partial.astype(BF16).reshape(rows, half, -1), "row")
        slope_mine = (both_grads * silu_slope(preact)).astype(BF16)
        slope = send_copies(slope_mine, "row")

        acts = jax.nn.silu(preact).astype(BF16)
        acts = either(h == k, acts[:, :width], acts[:, width:], 0).reshape(2, half, width)
        near = lax.ppermute(acts[0], ("row", "col"), collect)
        far = lax.ppermute(acts[1], ("row", "col"), collect_far)
        activation = either(k == 0, near, far, 0)

        partial_grad = lax.dot_general(
            slope, both_weights, (((1,), (1,)), ((), ())), preferred_element_type=F32
        ).astype(BF16)
        partial_grad, slope_late = lax.optimization_barrier((partial_grad, slope))
        grad_shares = lax.all_to_all(
            partial_grad.reshape(cols // 2, mine_b, -1),
            "col", 0, 0, axis_index_groups=cores,
        )

        features_all = jnp.concatenate([features, lax.ppermute(features, "col", swap)])
        slope_all = jnp.concatenate(
            [slope_late[:, :width], lax.ppermute(slope_late[:, width:], "col", swap)]
        )
        weight_grad = lax.dot_general(
            features_all, slope_all, (((0,), (0,)), ((), ())), preferred_element_type=F32
        )
        grad_shares, weight_grad = lax.optimization_barrier((grad_shares, weight_grad))
        feature_grad = jnp.sum(grad_shares.astype(F32), axis=0)
        return (activation, weight_grad, feature_grad)

    return shards


def solution(mesh):
    return jax.shard_map(
        make_shards(mesh.shape["row"], mesh.shape["col"]),
        mesh=mesh,
        in_specs=(P("col", None, None), P(), P("row", "col"), P("row", "col")),
        out_specs=(P("row", "col"), P("row", "col"), P("col", "row")),
        check_vma=False,
    )
```

```python
import jax
import jax.numpy as jnp
from jax import lax
from jax.experimental import pallas as pl
from jax.experimental.pallas import tpu as pltpu
from jax.sharding import PartitionSpec as P

BF16 = jnp.bfloat16
F32 = jnp.float32


def silu_slope(values):
    sig = jax.nn.sigmoid(values)
    return sig * (1.0 + values * (1.0 - sig))


def send_copies(part, axis, groups=None):
    size = len(groups[0]) if groups else lax.axis_size(axis)
    copies = jnp.broadcast_to(part[None], (size, *part.shape))
    got = lax.all_to_all(copies, axis, 0, 0, axis_index_groups=groups)
    return got.reshape(-1, got.shape[-1])


def send_shares(shares, axis, groups=None):
    got = lax.all_to_all(shares, axis, 0, 0, axis_index_groups=groups)
    return jnp.sum(got.astype(F32), axis=0)


def in_vmem(array):
    return pltpu.with_memory_space_constraint(array, pltpu.VMEM)


def forward_kernel(features, own, other, out):
    width = own.shape[1]
    out[:, :width] = jnp.dot(features[...], own[...], preferred_element_type=F32).astype(BF16)
    out[:, width:] = jnp.dot(features[...], other[...], preferred_element_type=F32).astype(BF16)


WHOLE = pl.BlockSpec(memory_space=pltpu.VMEM)


def times_weights(features, own, other, steps=2):
    (batch, depth), width = features.shape, own.shape[1]
    rows = batch // steps
    return pl.pallas_call(
        forward_kernel,
        out_shape=jax.ShapeDtypeStruct((batch, 2 * width), BF16),
        grid=(steps,),
        in_specs=[pl.BlockSpec((rows, depth), lambda i: (i, 0)), WHOLE, WHOLE],
        out_specs=pl.BlockSpec((rows, 2 * width), lambda i: (i, 0)),
        name="times_weights",
    )(features, in_vmem(own), in_vmem(other))


def backward_kernel(slope, own, other, out):
    width = own.shape[1]
    dims = (((1,), (1,)), ((), ()))
    total = lax.dot_general(slope[:, :width], own[...], dims, preferred_element_type=F32)
    total += lax.dot_general(slope[:, width:], other[...], dims, preferred_element_type=F32)
    out[...] = total.astype(BF16)


def times_weights_back(slope, own, other, steps=2):
    batch, (depth, width) = slope.shape[0], own.shape
    block = depth // steps
    return pl.pallas_call(
        backward_kernel,
        out_shape=jax.ShapeDtypeStruct((batch, depth), BF16),
        grid=(steps,),
        in_specs=[
            WHOLE,
            pl.BlockSpec((block, width), lambda i: (i, 0)),
            pl.BlockSpec((block, width), lambda i: (i, 0)),
        ],
        out_specs=pl.BlockSpec((batch, block), lambda i: (0, i)),
        name="times_weights_back",
    )(in_vmem(slope), own, other)


def either(flag, first, second, axis):
    return jnp.where(
        flag,
        jnp.concatenate([first, second], axis),
        jnp.concatenate([second, first], axis),
    )


def make_shards(rows, cols):
    cores = [list(range(core, cols, 2)) for core in range(2)]
    swap = [(c, c ^ 1) for c in range(cols)]
    spread, spread_far = [], []
    for row in range(rows):
        for col in range(cols):
            h, k = row % 2, col % 2
            spread.append((row * cols + col, (row - h + k) * cols + col - k + h))
            spread_far.append((row * cols + col, (row - h + 1 - k) * cols + col - k + h))
    collect = [(b, a) for a, b in spread]
    collect_far = [(b, a) for a, b in spread_far]

    def shards(embeddings, projection, weight, act_grad):
        mine_b, width = act_grad.shape
        half = mine_b // 2
        emb_rows = weight.shape[0] // projection.shape[1]
        emb_first = lax.axis_index("row") * emb_rows
        h, k = lax.axis_index("row") % 2, lax.axis_index("col") % 2

        mine_emb = lax.dynamic_slice_in_dim(embeddings, emb_first, emb_rows, 1)
        interaction = jnp.einsum(
            "bid,bmd->bim", mine_emb, embeddings, preferred_element_type=F32
        ).astype(BF16)
        local_features = jnp.einsum(
            "bim,mr->bir", interaction, projection, preferred_element_type=F32
        )
        local_features = local_features.astype(BF16).reshape(mine_b, -1)
        features = send_copies(local_features, "col", cores)

        other_weight = lax.ppermute(weight, "col", swap)
        halves = act_grad.reshape(2, half, width)
        near = lax.ppermute(
            lax.dynamic_index_in_dim(halves, k, 0, False), ("row", "col"), spread
        )
        far = lax.ppermute(
            lax.dynamic_index_in_dim(halves, 1 - k, 0, False), ("row", "col"), spread_far
        )
        both_grads = either(h == k, near, far, 1).astype(F32)

        partial = times_weights(features, weight, other_weight)
        preact = send_shares(partial.reshape(rows, half, -1), "row")
        slope_mine = (both_grads * silu_slope(preact)).astype(BF16)
        slope = send_copies(slope_mine, "row")

        acts = jax.nn.silu(preact).astype(BF16)
        acts = either(h == k, acts[:, :width], acts[:, width:], 0).reshape(2, half, width)
        near = lax.ppermute(acts[0], ("row", "col"), collect)
        far = lax.ppermute(acts[1], ("row", "col"), collect_far)
        activation = either(k == 0, near, far, 0)

        other_features = lax.ppermute(features, "col", swap)
        slope, activation, other_features = lax.optimization_barrier(
            (slope, activation, other_features)
        )
        partial_grad = times_weights_back(slope, weight, other_weight)
        partial_grad, slope_late = lax.optimization_barrier((partial_grad, slope))
        grad_shares = lax.all_to_all(
            partial_grad.reshape(cols // 2, mine_b, -1),
            "col", 0, 0, axis_index_groups=cores,
        )

        features_all = jnp.concatenate([features, other_features])
        gathered = [
            lax.all_gather(piece, "col", axis_index_groups=[[c, c + 1] for c in range(0, cols, 2)])
            for piece in jnp.split(slope_late[:, width:], 2)
        ]
        other_slope = jnp.concatenate([lax.dynamic_index_in_dim(g, 1 - k, 0, False) for g in gathered])
        slope_all = jnp.concatenate([slope_late[:, :width], other_slope])
        weight_grad = lax.dot_general(
            features_all, slope_all, (((0,), (0,)), ((), ())), preferred_element_type=F32
        )
        grad_shares, weight_grad = lax.optimization_barrier((grad_shares, weight_grad))
        feature_grad = jnp.sum(grad_shares.astype(F32), axis=0)
        return (activation, weight_grad, feature_grad)

    return shards


def solution(mesh):
    return jax.shard_map(
        make_shards(mesh.shape["row"], mesh.shape["col"]),
        mesh=mesh,
        in_specs=(P("col", None, None), P(), P("row", "col"), P("row", "col")),
        out_specs=(P("row", "col"), P("row", "col"), P("col", "row")),
        check_vma=False,
    )
```

```python
import jax
import jax.numpy as jnp
from jax import lax
from jax.experimental import pallas as pl
from jax.experimental.pallas import tpu as pltpu
from jax.sharding import PartitionSpec as P

BF16 = jnp.bfloat16
F32 = jnp.float32


def silu_slope(values):
    sig = jax.nn.sigmoid(values)
    return sig * (1.0 + values * (1.0 - sig))


def send_copies(part, axis, groups=None):
    size = len(groups[0]) if groups else lax.axis_size(axis)
    copies = jnp.broadcast_to(part[None], (size, *part.shape))
    got = lax.all_to_all(copies, axis, 0, 0, axis_index_groups=groups)
    return got.reshape(-1, got.shape[-1])


def in_vmem(array):
    return pltpu.with_memory_space_constraint(array, pltpu.VMEM)


WHOLE = pl.BlockSpec(memory_space=pltpu.VMEM)
ANY = pl.BlockSpec(memory_space=pl.ANY)
SCALAR = pl.BlockSpec(memory_space=pltpu.SMEM)


def fetch_other(core, pairs, other, sems):
    rows = other.shape[0] // len(pairs)
    copies = []
    for i, pair in enumerate(pairs):
        copies.append(
            pltpu.make_async_copy(
                pair.at[1 - core], other.at[pl.ds(i * rows, rows)], sems.at[i]
            )
        )
        copies[-1].start()
    return copies


def forward_kernel(core, features, own, *rest):
    *pairs, out, other, left, right, sems, out_sems = rest
    width = own.shape[1]
    copies = fetch_other(core[0], pairs, other, sems)
    left[...] = jnp.dot(features[...], own[...], preferred_element_type=F32).astype(BF16)
    send_left = pltpu.make_async_copy(left, out.at[:, pl.ds(0, width)], out_sems.at[0])
    send_left.start()
    for copy in copies:
        copy.wait()
    right[...] = jnp.dot(features[...], other[...], preferred_element_type=F32).astype(BF16)
    send_right = pltpu.make_async_copy(right, out.at[:, pl.ds(width, width)], out_sems.at[1])
    send_right.start()
    send_left.wait()
    send_right.wait()


def times_weights(core, features, own, pairs):
    batch, (depth, width) = features.shape[0], own.shape
    return pl.pallas_call(
        forward_kernel,
        out_shape=jax.ShapeDtypeStruct((batch, 2 * width), BF16),
        in_specs=[SCALAR, WHOLE, WHOLE] + [ANY] * len(pairs),
        out_specs=ANY,
        scratch_shapes=[
            pltpu.VMEM((depth, width), BF16),
            pltpu.VMEM((batch, width), BF16),
            pltpu.VMEM((batch, width), BF16),
            pltpu.SemaphoreType.DMA((len(pairs),)),
            pltpu.SemaphoreType.DMA((2,)),
        ],
        name="times_weights",
    )(core, in_vmem(features), in_vmem(own), *pairs)


def backward_kernel(core, slope, own_in, *rest):
    *pairs, out, first, second, own, other, sems, own_sems, out_sems = rest
    width, rows = own.shape[1], own.shape[0] // len(pairs)
    half = first.shape[0]
    own_copies = []
    for i in range(len(pairs)):
        piece = pl.ds(i * rows, rows)
        own_copies.append(
            pltpu.make_async_copy(own_in.at[piece], own.at[piece], own_sems.at[i])
        )
        own_copies[-1].start()
    copies = fetch_other(core[0], pairs, other, sems)
    gives = [
        pltpu.make_async_copy(
            slope.at[pl.ds(i * half, half), pl.ds(width, width)], give, out_sems.at[i]
        )
        for i, give in enumerate((first, second))
    ]
    for give in gives:
        give.start()
    dims = (((1,), (1,)), ((), ()))
    for i in range(0, len(pairs), 2):
        piece = pl.ds(i * rows, 2 * rows)
        for copy in own_copies[i : i + 2] + copies[i : i + 2]:
            copy.wait()
        total = lax.dot_general(
            slope[:, :width], own[piece], dims, preferred_element_type=F32
        ) + lax.dot_general(
            slope[:, width:], other[piece], dims, preferred_element_type=F32
        )
        out[:, piece] = total.astype(BF16)
    for give in gives:
        give.wait()


def times_weights_back(core, slope, own, pairs):
    batch, (depth, width) = slope.shape[0], own.shape
    return pl.pallas_call(
        backward_kernel,
        out_shape=[jax.ShapeDtypeStruct((batch, depth), BF16)]
        + [jax.ShapeDtypeStruct((batch // 2, width), BF16)] * 2,
        in_specs=[SCALAR, WHOLE, ANY] + [ANY] * len(pairs),
        out_specs=[WHOLE, ANY, ANY],
        scratch_shapes=[
            pltpu.VMEM((depth, width), BF16),
            pltpu.VMEM((depth, width), BF16),
            pltpu.SemaphoreType.DMA((len(pairs),)),
            pltpu.SemaphoreType.DMA((len(pairs),)),
            pltpu.SemaphoreType.DMA((2,)),
        ],
        name="times_weights_back",
    )(core, in_vmem(slope), own, *pairs)


def weight_grad_kernel(core, features, other_features, slope, *rest):
    *pairs, out, other, sems = rest
    width = other.shape[1]
    copies = fetch_other(core[0], pairs, other, sems)
    for copy in copies:
        copy.wait()
    dims = (((0,), (0,)), ((), ()))
    out[...] = lax.dot_general(
        features[...], slope[:, :width], dims, preferred_element_type=F32
    ) + lax.dot_general(
        other_features[...], other[...], dims, preferred_element_type=F32
    )


def weight_grad_of(core, features, other_features, slope, pairs):
    depth, (batch, both) = features.shape[1], slope.shape
    return pl.pallas_call(
        weight_grad_kernel,
        out_shape=jax.ShapeDtypeStruct((depth, both // 2), F32),
        in_specs=[SCALAR, WHOLE, WHOLE, WHOLE] + [ANY] * len(pairs),
        out_specs=WHOLE,
        scratch_shapes=[
            pltpu.VMEM((batch, both // 2), BF16),
            pltpu.SemaphoreType.DMA((len(pairs),)),
        ],
        name="weight_grad",
    )(core, features, other_features, in_vmem(slope), *pairs)


def activate_kernel(shares, grads, acts, copies, slope, sem):
    preact = shares[0].astype(F32)
    for i in range(1, shares.shape[0]):
        preact += shares[i].astype(F32)
    acts[...] = jax.nn.silu(preact).astype(BF16)
    slope[...] = (grads[...].astype(F32) * silu_slope(preact)).astype(BF16)
    sends = [
        pltpu.make_async_copy(slope, copies.at[i], sem.at[i])
        for i in range(copies.shape[0])
    ]
    for send in sends:
        send.start()
    for send in sends:
        send.wait()


def activate(shares, grads):
    return pl.pallas_call(
        activate_kernel,
        out_shape=[
            jax.ShapeDtypeStruct(shares.shape[1:], BF16),
            jax.ShapeDtypeStruct(shares.shape, BF16),
        ],
        in_specs=[WHOLE, WHOLE],
        out_specs=[WHOLE, ANY],
        scratch_shapes=[
            pltpu.VMEM(shares.shape[1:], BF16),
            pltpu.SemaphoreType.DMA((shares.shape[0],)),
        ],
        name="activate",
    )(in_vmem(shares), in_vmem(grads))


def either(flag, first, second, axis):
    return jnp.where(
        flag,
        jnp.concatenate([first, second], axis),
        jnp.concatenate([second, first], axis),
    )


def make_shards(rows, cols):
    cores = [list(range(core, cols, 2)) for core in range(2)]
    chips = [[c, c + 1] for c in range(0, cols, 2)]
    swap = [(c, c ^ 1) for c in range(cols)]
    spread, spread_far = [], []
    for row in range(rows):
        for col in range(cols):
            h, k = row % 2, col % 2
            spread.append((row * cols + col, (row - h + k) * cols + col - k + h))
            spread_far.append((row * cols + col, (row - h + 1 - k) * cols + col - k + h))
    collect = [(b, a) for a, b in spread]
    collect_far = [(b, a) for a, b in spread_far]

    def shards(embeddings, projection, weight, act_grad):
        mine_b, width = act_grad.shape
        half = mine_b // 2
        emb_rows = weight.shape[0] // projection.shape[1]
        emb_first = lax.axis_index("row") * emb_rows
        h, k = lax.axis_index("row") % 2, lax.axis_index("col") % 2

        mine_emb = lax.dynamic_slice_in_dim(embeddings, emb_first, emb_rows, 1)
        interaction = jnp.einsum(
            "bid,bmd->bim", mine_emb, embeddings, preferred_element_type=F32
        ).astype(BF16)
        local_features = jnp.einsum(
            "bim,mr->bir", interaction, projection, preferred_element_type=F32
        )
        local_features = local_features.astype(BF16).reshape(mine_b, -1)
        features = send_copies(local_features, "col", cores)

        weight_pairs = [
            lax.all_gather(piece, "col", axis_index_groups=chips)
            for piece in jnp.split(weight, 4)
        ]
        core = k.reshape(1)
        halves = act_grad.reshape(2, half, width)
        near = lax.ppermute(
            lax.dynamic_index_in_dim(halves, k, 0, False), ("row", "col"), spread
        )
        far = lax.ppermute(
            lax.dynamic_index_in_dim(halves, 1 - k, 0, False), ("row", "col"), spread_far
        )
        both_grads = either(h == k, near, far, 1)

        partial = times_weights(core, features, weight, weight_pairs)
        shares = lax.all_to_all(partial.reshape(rows, half, -1), "row", 0, 0)
        acts, slope_copies = activate(shares, both_grads)
        slope = lax.all_to_all(slope_copies, "row", 0, 0).reshape(rows * half, -1)

        acts = either(h == k, acts[:, :width], acts[:, width:], 0).reshape(2, half, width)
        near = lax.ppermute(acts[0], ("row", "col"), collect)
        far = lax.ppermute(acts[1], ("row", "col"), collect_far)
        activation = either(k == 0, near, far, 0)

        other_features = lax.ppermute(features, "col", swap)
        slope, activation, other_features = lax.optimization_barrier(
            (slope, activation, other_features)
        )
        partial_grad, *given = times_weights_back(core, slope, weight, weight_pairs)
        grad_shares = lax.all_to_all(
            partial_grad.reshape(cols // 2, mine_b, -1),
            "col", 0, 0, axis_index_groups=cores,
        )

        slope_pairs = [
            lax.all_gather(piece, "col", axis_index_groups=chips) for piece in given
        ]
        weight_grad = weight_grad_of(core, features, other_features, slope, slope_pairs)
        grad_shares, weight_grad = lax.optimization_barrier((grad_shares, weight_grad))
        feature_grad = jnp.sum(grad_shares.astype(F32), axis=0)
        return (activation, weight_grad, feature_grad)

    return shards


def solution(mesh):
    return jax.shard_map(
        make_shards(mesh.shape["row"], mesh.shape["col"]),
        mesh=mesh,
        in_specs=(P("col", None, None), P(), P("row", "col"), P("row", "col")),
        out_specs=(P("row", "col"), P("row", "col"), P("col", "row")),
        check_vma=False,
    )
```

```python
import jax
import jax.numpy as jnp
from jax import lax
from jax.experimental import pallas as pl
from jax.experimental.pallas import tpu as pltpu
from jax.sharding import PartitionSpec as P

BF16 = jnp.bfloat16
F32 = jnp.float32


def silu_slope(values):
    sig = jax.nn.sigmoid(values)
    return sig * (1.0 + values * (1.0 - sig))


def send_copies(part, axis, groups=None):
    size = len(groups[0]) if groups else lax.axis_size(axis)
    copies = jnp.broadcast_to(part[None], (size, *part.shape))
    got = lax.all_to_all(copies, axis, 0, 0, axis_index_groups=groups)
    return got.reshape(-1, got.shape[-1])


def send_shares(shares, axis, groups=None):
    got = lax.all_to_all(shares, axis, 0, 0, axis_index_groups=groups)
    return jnp.sum(got.astype(F32), axis=0)


def in_vmem(array):
    return pltpu.with_memory_space_constraint(array, pltpu.VMEM)


WHOLE = pl.BlockSpec(memory_space=pltpu.VMEM)


def forward_kernel(features, own, other, out):
    step, block = pl.program_id(0), out.shape[1]
    for i in range(2 * own.shape[1] // block):
        weight, first = (own, i * block) if i * block < own.shape[1] else (other, i * block - own.shape[1])

        @pl.when(step == i)
        def _(weight=weight, first=first):
            part = weight[:, first : first + block]
            out[...] = jnp.dot(features[...], part, preferred_element_type=F32).astype(BF16)


def times_weights(features, own, other, blocks=2):
    (batch, depth), width = features.shape, own.shape[1]
    block = width // blocks
    return pl.pallas_call(
        forward_kernel,
        out_shape=jax.ShapeDtypeStruct((batch, 2 * width), BF16),
        grid=(2 * blocks,),
        in_specs=[
            pl.BlockSpec((batch, depth), lambda i: (0, 0)),
            WHOLE,
            WHOLE,
        ],
        out_specs=pl.BlockSpec((batch, block), lambda i: (0, i)),
        name="times_weights",
    )(features, in_vmem(own), in_vmem(other))


def backward_kernel(slope, own, other, out):
    width, block = own.shape[1], out.shape[1]
    mine = own[pl.ds(pl.multiple_of(pl.program_id(0) * block, block), block)]
    dims = (((1,), (1,)), ((), ()))
    total = lax.dot_general(slope[:, :width], mine, dims, preferred_element_type=F32)
    total += lax.dot_general(slope[:, width:], other[...], dims, preferred_element_type=F32)
    out[...] = total.astype(BF16)


def times_weights_back(slope, own, other, steps=2):
    batch, (depth, width) = slope.shape[0], own.shape
    block = depth // steps
    return pl.pallas_call(
        backward_kernel,
        out_shape=jax.ShapeDtypeStruct((batch, depth), BF16),
        grid=(steps,),
        in_specs=[
            WHOLE,
            WHOLE,
            pl.BlockSpec((block, width), lambda i: (i, 0)),
        ],
        out_specs=pl.BlockSpec((batch, block), lambda i: (0, i)),
        name="times_weights_back",
    )(in_vmem(slope), in_vmem(own), other)


def either(flag, first, second, axis):
    return jnp.where(
        flag,
        jnp.concatenate([first, second], axis),
        jnp.concatenate([second, first], axis),
    )


def make_shards(rows, cols):
    cores = [list(range(core, cols, 2)) for core in range(2)]
    swap = [(c, c ^ 1) for c in range(cols)]
    spread, spread_far = [], []
    for row in range(rows):
        for col in range(cols):
            h, k = row % 2, col % 2
            spread.append((row * cols + col, (row - h + k) * cols + col - k + h))
            spread_far.append((row * cols + col, (row - h + 1 - k) * cols + col - k + h))
    collect = [(b, a) for a, b in spread]
    collect_far = [(b, a) for a, b in spread_far]

    def shards(embeddings, projection, weight, act_grad):
        mine_b, width = act_grad.shape
        half = mine_b // 2
        emb_rows = weight.shape[0] // projection.shape[1]
        emb_first = lax.axis_index("row") * emb_rows
        h, k = lax.axis_index("row") % 2, lax.axis_index("col") % 2

        mine_emb = lax.dynamic_slice_in_dim(embeddings, emb_first, emb_rows, 1)
        interaction = jnp.einsum(
            "bid,bmd->bim", mine_emb, embeddings, preferred_element_type=F32
        ).astype(BF16)
        local_features = jnp.einsum(
            "bim,mr->bir", interaction, projection, preferred_element_type=F32
        )
        local_features = local_features.astype(BF16).reshape(mine_b, -1)
        features = send_copies(local_features, "col", cores)

        other_weight = lax.ppermute(weight, "col", swap)
        halves = act_grad.reshape(2, half, width)
        near = lax.ppermute(
            lax.dynamic_index_in_dim(halves, k, 0, False), ("row", "col"), spread
        )
        far = lax.ppermute(
            lax.dynamic_index_in_dim(halves, 1 - k, 0, False), ("row", "col"), spread_far
        )
        both_grads = either(h == k, near, far, 1).astype(F32)

        partial = times_weights(features, weight, other_weight)
        preact = send_shares(partial.reshape(rows, half, -1), "row")
        slope_mine = (both_grads * silu_slope(preact)).astype(BF16)
        slope = send_copies(slope_mine, "row")

        acts = jax.nn.silu(preact).astype(BF16)
        acts = either(h == k, acts[:, :width], acts[:, width:], 0).reshape(2, half, width)
        near = lax.ppermute(acts[0], ("row", "col"), collect)
        far = lax.ppermute(acts[1], ("row", "col"), collect_far)
        activation = either(k == 0, near, far, 0)

        other_features = lax.ppermute(features, "col", swap)
        slope, activation, other_features = lax.optimization_barrier(
            (slope, activation, other_features)
        )
        partial_grad = times_weights_back(slope, weight, other_weight)
        partial_grad, slope_late = lax.optimization_barrier((partial_grad, slope))
        grad_shares = lax.all_to_all(
            partial_grad.reshape(cols // 2, mine_b, -1),
            "col", 0, 0, axis_index_groups=cores,
        )

        features_all = jnp.concatenate([features, other_features])
        gathered = [
            lax.all_gather(piece, "col", axis_index_groups=[[c, c + 1] for c in range(0, cols, 2)])
            for piece in jnp.split(slope_late[:, width:], 2)
        ]
        other_slope = jnp.concatenate([lax.dynamic_index_in_dim(g, 1 - k, 0, False) for g in gathered])
        slope_all = jnp.concatenate([slope_late[:, :width], other_slope])
        weight_grad = lax.dot_general(
            features_all, slope_all, (((0,), (0,)), ((), ())), preferred_element_type=F32
        )
        grad_shares, weight_grad = lax.optimization_barrier((grad_shares, weight_grad))
        feature_grad = jnp.sum(grad_shares.astype(F32), axis=0)
        return (activation, weight_grad, feature_grad)

    return shards


def solution(mesh):
    return jax.shard_map(
        make_shards(mesh.shape["row"], mesh.shape["col"]),
        mesh=mesh,
        in_specs=(P("col", None, None), P(), P("row", "col"), P("row", "col")),
        out_specs=(P("row", "col"), P("row", "col"), P("col", "row")),
        check_vma=False,
    )
```

```python
import jax
import jax.numpy as jnp
from jax import lax
from jax.experimental import pallas as pl
from jax.experimental.pallas import tpu as pltpu
from jax.sharding import PartitionSpec as P

BF16 = jnp.bfloat16
F32 = jnp.float32


def silu_slope(values):
    sig = jax.nn.sigmoid(values)
    return sig * (1.0 + values * (1.0 - sig))


def send_copies(part, axis, groups=None):
    size = len(groups[0]) if groups else lax.axis_size(axis)
    copies = jnp.broadcast_to(part[None], (size, *part.shape))
    got = lax.all_to_all(copies, axis, 0, 0, axis_index_groups=groups)
    return got.reshape(-1, got.shape[-1])


def send_shares(shares, axis, groups=None):
    got = lax.all_to_all(shares, axis, 0, 0, axis_index_groups=groups)
    return jnp.sum(got.astype(F32), axis=0)


def in_vmem(array):
    return pltpu.with_memory_space_constraint(array, pltpu.VMEM)


WHOLE = pl.BlockSpec(memory_space=pltpu.VMEM)


def forward_kernel(features, own, other, out):
    width, rows = own.shape[1], out.shape[0]
    mine = features[pl.ds(pl.multiple_of(pl.program_id(0) * rows, rows), rows)]
    out[:, :width] = jnp.dot(mine, own[...], preferred_element_type=F32).astype(BF16)
    out[:, width:] = jnp.dot(mine, other[...], preferred_element_type=F32).astype(BF16)


def times_weights(features, own, other, steps=2):
    batch, width = features.shape[0], own.shape[1]
    return pl.pallas_call(
        forward_kernel,
        out_shape=jax.ShapeDtypeStruct((batch, 2 * width), BF16),
        grid=(steps,),
        in_specs=[WHOLE, WHOLE, WHOLE],
        out_specs=pl.BlockSpec((batch // steps, 2 * width), lambda i: (i, 0)),
        name="times_weights",
    )(in_vmem(features), in_vmem(own), in_vmem(other))


def backward_kernel(slope, own, other, out):
    width, block = own.shape[1], out.shape[1]
    mine = own[pl.ds(pl.multiple_of(pl.program_id(0) * block, block), block)]
    dims = (((1,), (1,)), ((), ()))
    total = lax.dot_general(slope[:, :width], mine, dims, preferred_element_type=F32)
    total += lax.dot_general(slope[:, width:], other[...], dims, preferred_element_type=F32)
    out[...] = total.astype(BF16)


def times_weights_back(slope, own, other, steps=2):
    batch, (depth, width) = slope.shape[0], own.shape
    block = depth // steps
    return pl.pallas_call(
        backward_kernel,
        out_shape=jax.ShapeDtypeStruct((batch, depth), BF16),
        grid=(steps,),
        in_specs=[
            WHOLE,
            WHOLE,
            pl.BlockSpec((block, width), lambda i: (i, 0)),
        ],
        out_specs=pl.BlockSpec((batch, block), lambda i: (0, i)),
        name="times_weights_back",
    )(in_vmem(slope), in_vmem(own), other)


def either(flag, first, second, axis):
    return jnp.where(
        flag,
        jnp.concatenate([first, second], axis),
        jnp.concatenate([second, first], axis),
    )


def make_shards(rows, cols):
    cores = [list(range(core, cols, 2)) for core in range(2)]
    swap = [(c, c ^ 1) for c in range(cols)]
    spread, spread_far = [], []
    for row in range(rows):
        for col in range(cols):
            h, k = row % 2, col % 2
            spread.append((row * cols + col, (row - h + k) * cols + col - k + h))
            spread_far.append((row * cols + col, (row - h + 1 - k) * cols + col - k + h))
    collect = [(b, a) for a, b in spread]
    collect_far = [(b, a) for a, b in spread_far]

    def shards(embeddings, projection, weight, act_grad):
        mine_b, width = act_grad.shape
        half = mine_b // 2
        emb_rows = weight.shape[0] // projection.shape[1]
        emb_first = lax.axis_index("row") * emb_rows
        h, k = lax.axis_index("row") % 2, lax.axis_index("col") % 2

        mine_emb = lax.dynamic_slice_in_dim(embeddings, emb_first, emb_rows, 1)
        interaction = jnp.einsum(
            "bid,bmd->bim", mine_emb, embeddings, preferred_element_type=F32
        ).astype(BF16)
        local_features = jnp.einsum(
            "bim,mr->bir", interaction, projection, preferred_element_type=F32
        )
        local_features = local_features.astype(BF16).reshape(mine_b, -1)
        local_features, own = lax.optimization_barrier((local_features, weight))
        features = send_copies(local_features, "col", cores)

        other_weight = lax.ppermute(weight, "col", swap)
        halves = act_grad.reshape(2, half, width)
        near = lax.ppermute(
            lax.dynamic_index_in_dim(halves, k, 0, False), ("row", "col"), spread
        )
        far = lax.ppermute(
            lax.dynamic_index_in_dim(halves, 1 - k, 0, False), ("row", "col"), spread_far
        )
        both_grads = either(h == k, near, far, 1).astype(F32)

        partial = times_weights(features, own, other_weight)
        preact = send_shares(partial.reshape(rows, half, -1), "row")
        slope_mine = (both_grads * silu_slope(preact)).astype(BF16)
        slope = send_copies(slope_mine, "row")

        acts = jax.nn.silu(preact).astype(BF16)
        acts = either(h == k, acts[:, :width], acts[:, width:], 0).reshape(2, half, width)
        near = lax.ppermute(acts[0], ("row", "col"), collect)
        far = lax.ppermute(acts[1], ("row", "col"), collect_far)
        activation = either(k == 0, near, far, 0)

        other_features = lax.ppermute(features, "col", swap)
        slope, activation, other_features = lax.optimization_barrier(
            (slope, activation, other_features)
        )
        partial_grad = times_weights_back(slope, own, other_weight)
        partial_grad, slope_late = lax.optimization_barrier((partial_grad, slope))
        grad_shares = lax.all_to_all(
            partial_grad.reshape(cols // 2, mine_b, -1),
            "col", 0, 0, axis_index_groups=cores,
        )

        features_all = jnp.concatenate([features, other_features])
        gathered = [
            lax.all_gather(piece, "col", axis_index_groups=[[c, c + 1] for c in range(0, cols, 2)])
            for piece in jnp.split(slope_late[:, width:], 2)
        ]
        other_slope = jnp.concatenate([lax.dynamic_index_in_dim(g, 1 - k, 0, False) for g in gathered])
        slope_all = jnp.concatenate([slope_late[:, :width], other_slope])
        weight_grad = lax.dot_general(
            features_all, slope_all, (((0,), (0,)), ((), ())), preferred_element_type=F32
        )
        grad_shares, weight_grad = lax.optimization_barrier((grad_shares, weight_grad))
        feature_grad = jnp.sum(grad_shares.astype(F32), axis=0)
        return (activation, weight_grad, feature_grad)

    return shards


def solution(mesh):
    return jax.shard_map(
        make_shards(mesh.shape["row"], mesh.shape["col"]),
        mesh=mesh,
        in_specs=(P("col", None, None), P(), P("row", "col"), P("row", "col")),
        out_specs=(P("row", "col"), P("row", "col"), P("col", "row")),
        check_vma=False,
    )
```

```python
import jax
import jax.numpy as jnp
from jax import lax
from jax.experimental import pallas as pl
from jax.experimental.pallas import tpu as pltpu
from jax.sharding import PartitionSpec as P

BF16 = jnp.bfloat16
F32 = jnp.float32
WEIGHT_PIECES = 4


def silu_slope(values):
    sig = jax.nn.sigmoid(values)
    return sig * (1.0 + values * (1.0 - sig))


def send_copies(part, axis, groups=None):
    size = len(groups[0]) if groups else lax.axis_size(axis)
    copies = jnp.broadcast_to(part[None], (size, *part.shape))
    got = lax.all_to_all(copies, axis, 0, 0, axis_index_groups=groups)
    return got.reshape(-1, got.shape[-1])


def send_shares(shares, axis, groups=None):
    got = lax.all_to_all(shares, axis, 0, 0, axis_index_groups=groups)
    return jnp.sum(got.astype(F32), axis=0)


def in_vmem(array):
    return pltpu.with_memory_space_constraint(array, pltpu.VMEM)


WHOLE = pl.BlockSpec(memory_space=pltpu.VMEM)


def forward_kernel(features, own, *rest):
    *others, out = rest
    width, rows = own.shape[1], out.shape[0]
    mine = features[pl.ds(pl.multiple_of(pl.program_id(0) * rows, rows), rows)]
    out[:, :width] = jnp.dot(mine, own[...], preferred_element_type=F32).astype(BF16)
    first = width
    for other in others:
        part = jnp.dot(mine, other[...], preferred_element_type=F32)
        out[:, first : first + other.shape[1]] = part.astype(BF16)
        first += other.shape[1]


def times_weights(features, own, others, steps=2):
    batch, width = features.shape[0], own.shape[1]
    return pl.pallas_call(
        forward_kernel,
        out_shape=jax.ShapeDtypeStruct((batch, 2 * width), BF16),
        grid=(steps,),
        in_specs=[WHOLE] * (2 + len(others)),
        out_specs=pl.BlockSpec((batch // steps, 2 * width), lambda i: (i, 0)),
        name="times_weights",
    )(in_vmem(features), in_vmem(own), *map(in_vmem, others))


def backward_kernel(slope, own, *rest):
    *others, out = rest
    width, block = own.shape[1], out.shape[1]
    mine = own[pl.ds(pl.multiple_of(pl.program_id(0) * block, block), block)]
    dims = (((1,), (1,)), ((), ()))
    total = lax.dot_general(slope[:, :width], mine, dims, preferred_element_type=F32)
    first = width
    for other in others:
        part = slope[:, first : first + other.shape[1]]
        total += lax.dot_general(part, other[...], dims, preferred_element_type=F32)
        first += other.shape[1]
    out[...] = total.astype(BF16)


def times_weights_back(slope, own, others, steps=2):
    batch, depth = slope.shape[0], own.shape[0]
    block = depth // steps
    return pl.pallas_call(
        backward_kernel,
        out_shape=jax.ShapeDtypeStruct((batch, depth), BF16),
        grid=(steps,),
        in_specs=[WHOLE, WHOLE]
        + [pl.BlockSpec((block, other.shape[1]), lambda i: (i, 0)) for other in others],
        out_specs=pl.BlockSpec((batch, block), lambda i: (0, i)),
        name="times_weights_back",
    )(in_vmem(slope), in_vmem(own), *others)


def either(flag, first, second, axis):
    return jnp.where(
        flag,
        jnp.concatenate([first, second], axis),
        jnp.concatenate([second, first], axis),
    )


def make_shards(rows, cols):
    cores = [list(range(core, cols, 2)) for core in range(2)]
    swap = [(c, c ^ 1) for c in range(cols)]
    spread, spread_far = [], []
    for row in range(rows):
        for col in range(cols):
            h, k = row % 2, col % 2
            spread.append((row * cols + col, (row - h + k) * cols + col - k + h))
            spread_far.append((row * cols + col, (row - h + 1 - k) * cols + col - k + h))
    collect = [(b, a) for a, b in spread]
    collect_far = [(b, a) for a, b in spread_far]

    def shards(embeddings, projection, weight, act_grad):
        mine_b, width = act_grad.shape
        half = mine_b // 2
        emb_rows = weight.shape[0] // projection.shape[1]
        emb_first = lax.axis_index("row") * emb_rows
        h, k = lax.axis_index("row") % 2, lax.axis_index("col") % 2

        mine_emb = lax.dynamic_slice_in_dim(embeddings, emb_first, emb_rows, 1)
        interaction = jnp.einsum(
            "bid,bmd->bim", mine_emb, embeddings, preferred_element_type=F32
        ).astype(BF16)
        local_features = jnp.einsum(
            "bim,mr->bir", interaction, projection, preferred_element_type=F32
        )
        local_features = local_features.astype(BF16).reshape(mine_b, -1)
        local_features, late_weight = lax.optimization_barrier((local_features, weight))
        own = weight
        features = send_copies(local_features, "col", cores)

        other_weight = [
            lax.ppermute(piece, "col", swap) for piece in jnp.split(late_weight, WEIGHT_PIECES, axis=1)
        ]
        halves = act_grad.reshape(2, half, width)
        near = lax.ppermute(
            lax.dynamic_index_in_dim(halves, k, 0, False), ("row", "col"), spread
        )
        far = lax.ppermute(
            lax.dynamic_index_in_dim(halves, 1 - k, 0, False), ("row", "col"), spread_far
        )
        both_grads = either(h == k, near, far, 1).astype(F32)

        partial = times_weights(features, own, other_weight)
        preact = send_shares(partial.reshape(rows, half, -1), "row")
        slope_mine = (both_grads * silu_slope(preact)).astype(BF16)
        slope = send_copies(slope_mine, "row")

        acts = jax.nn.silu(preact).astype(BF16)
        acts = either(h == k, acts[:, :width], acts[:, width:], 0).reshape(2, half, width)
        near = lax.ppermute(acts[0], ("row", "col"), collect)
        far = lax.ppermute(acts[1], ("row", "col"), collect_far)
        activation = either(k == 0, near, far, 0)

        other_features = lax.ppermute(features, "col", swap)
        slope, activation, other_features = lax.optimization_barrier(
            (slope, activation, other_features)
        )
        partial_grad = times_weights_back(slope, own, other_weight)
        partial_grad, slope_late = lax.optimization_barrier((partial_grad, slope))
        grad_shares = lax.all_to_all(
            partial_grad.reshape(cols // 2, mine_b, -1),
            "col", 0, 0, axis_index_groups=cores,
        )

        features_all = jnp.concatenate([features, other_features])
        gathered = [
            lax.all_gather(piece, "col", axis_index_groups=[[c, c + 1] for c in range(0, cols, 2)])
            for piece in jnp.split(slope_late[:, width:], 2)
        ]
        other_slope = jnp.concatenate([lax.dynamic_index_in_dim(g, 1 - k, 0, False) for g in gathered])
        slope_all = jnp.concatenate([slope_late[:, :width], other_slope])
        weight_grad = lax.dot_general(
            features_all, slope_all, (((0,), (0,)), ((), ())), preferred_element_type=F32
        )
        grad_shares, weight_grad = lax.optimization_barrier((grad_shares, weight_grad))
        feature_grad = jnp.sum(grad_shares.astype(F32), axis=0)
        return (activation, weight_grad, feature_grad)

    return shards


def solution(mesh):
    return jax.shard_map(
        make_shards(mesh.shape["row"], mesh.shape["col"]),
        mesh=mesh,
        in_specs=(P("col", None, None), P(), P("row", "col"), P("row", "col")),
        out_specs=(P("row", "col"), P("row", "col"), P("col", "row")),
        check_vma=False,
    )
```

```python
import jax
import jax.numpy as jnp
from jax import lax
from jax.experimental import pallas as pl
from jax.experimental.pallas import tpu as pltpu
from jax.sharding import PartitionSpec as P

BF16 = jnp.bfloat16
F32 = jnp.float32
WEIGHT_CUTS = (384, 768)


def silu_slope(values):
    sig = jax.nn.sigmoid(values)
    return sig * (1.0 + values * (1.0 - sig))


def send_copies(part, axis, groups=None):
    size = len(groups[0]) if groups else lax.axis_size(axis)
    copies = jnp.broadcast_to(part[None], (size, *part.shape))
    got = lax.all_to_all(copies, axis, 0, 0, axis_index_groups=groups)
    return got.reshape(-1, got.shape[-1])


def send_shares(shares, axis, groups=None):
    got = lax.all_to_all(shares, axis, 0, 0, axis_index_groups=groups)
    return jnp.sum(got.astype(F32), axis=0)


def in_vmem(array):
    return pltpu.with_memory_space_constraint(array, pltpu.VMEM)


WHOLE = pl.BlockSpec(memory_space=pltpu.VMEM)


def forward_kernel(features, own, *rest):
    *others, out = rest
    width, rows = own.shape[1], out.shape[0]
    mine = features[pl.ds(pl.multiple_of(pl.program_id(0) * rows, rows), rows)]
    out[:, :width] = jnp.dot(mine, own[...], preferred_element_type=F32).astype(BF16)
    first = width
    for other in others:
        part = jnp.dot(mine, other[...], preferred_element_type=F32)
        out[:, first : first + other.shape[1]] = part.astype(BF16)
        first += other.shape[1]


def times_weights(features, own, others, steps=2):
    batch, width = features.shape[0], own.shape[1]
    return pl.pallas_call(
        forward_kernel,
        out_shape=jax.ShapeDtypeStruct((batch, 2 * width), BF16),
        grid=(steps,),
        in_specs=[WHOLE] * (2 + len(others)),
        out_specs=pl.BlockSpec((batch // steps, 2 * width), lambda i: (i, 0)),
        name="times_weights",
    )(in_vmem(features), in_vmem(own), *map(in_vmem, others))


def backward_kernel(slope, own, *rest):
    *others, out = rest
    width, block = own.shape[1], out.shape[1]
    mine = own[pl.ds(pl.multiple_of(pl.program_id(0) * block, block), block)]
    dims = (((1,), (1,)), ((), ()))
    total = lax.dot_general(slope[:, :width], mine, dims, preferred_element_type=F32)
    first = width
    for other in others:
        part = slope[:, first : first + other.shape[1]]
        total += lax.dot_general(part, other[...], dims, preferred_element_type=F32)
        first += other.shape[1]
    out[...] = total.astype(BF16)


def times_weights_back(slope, own, others, steps=2):
    batch, depth = slope.shape[0], own.shape[0]
    block = depth // steps
    return pl.pallas_call(
        backward_kernel,
        out_shape=jax.ShapeDtypeStruct((batch, depth), BF16),
        grid=(steps,),
        in_specs=[WHOLE, WHOLE]
        + [pl.BlockSpec((block, other.shape[1]), lambda i: (i, 0)) for other in others],
        out_specs=pl.BlockSpec((batch, block), lambda i: (0, i)),
        name="times_weights_back",
    )(in_vmem(slope), in_vmem(own), *others)


def either(flag, first, second, axis):
    return jnp.where(
        flag,
        jnp.concatenate([first, second], axis),
        jnp.concatenate([second, first], axis),
    )


def make_shards(rows, cols):
    cores = [list(range(core, cols, 2)) for core in range(2)]
    swap = [(c, c ^ 1) for c in range(cols)]
    spread, spread_far = [], []
    for row in range(rows):
        for col in range(cols):
            h, k = row % 2, col % 2
            spread.append((row * cols + col, (row - h + k) * cols + col - k + h))
            spread_far.append((row * cols + col, (row - h + 1 - k) * cols + col - k + h))
    collect = [(b, a) for a, b in spread]
    collect_far = [(b, a) for a, b in spread_far]

    def shards(embeddings, projection, weight, act_grad):
        mine_b, width = act_grad.shape
        half = mine_b // 2
        emb_rows = weight.shape[0] // projection.shape[1]
        emb_first = lax.axis_index("row") * emb_rows
        h, k = lax.axis_index("row") % 2, lax.axis_index("col") % 2

        mine_emb = lax.dynamic_slice_in_dim(embeddings, emb_first, emb_rows, 1)
        interaction = jnp.einsum(
            "bid,bmd->bim", mine_emb, embeddings, preferred_element_type=F32
        ).astype(BF16)
        local_features = jnp.einsum(
            "bim,mr->bir", interaction, projection, preferred_element_type=F32
        )
        local_features = local_features.astype(BF16).reshape(mine_b, -1)
        local_features, late_weight = lax.optimization_barrier((local_features, weight))
        own = weight
        features = send_copies(local_features, "col", cores)

        other_weight = [
            lax.ppermute(piece, "col", swap) for piece in jnp.split(late_weight, WEIGHT_CUTS, axis=1)
        ]
        halves = act_grad.reshape(2, half, width)
        near = lax.ppermute(
            lax.dynamic_index_in_dim(halves, k, 0, False), ("row", "col"), spread
        )
        far = lax.ppermute(
            lax.dynamic_index_in_dim(halves, 1 - k, 0, False), ("row", "col"), spread_far
        )
        both_grads = either(h == k, near, far, 1).astype(F32)

        partial = times_weights(features, own, other_weight)
        preact = send_shares(partial.reshape(rows, half, -1), "row")
        slope_mine = (both_grads * silu_slope(preact)).astype(BF16)
        slope = send_copies(slope_mine, "row")

        acts = jax.nn.silu(preact).astype(BF16)
        acts = either(h == k, acts[:, :width], acts[:, width:], 0).reshape(2, half, width)
        near = lax.ppermute(acts[0], ("row", "col"), collect)
        far = lax.ppermute(acts[1], ("row", "col"), collect_far)
        activation = either(k == 0, near, far, 0)

        other_features = lax.ppermute(features, "col", swap)
        slope, activation, other_features = lax.optimization_barrier(
            (slope, activation, other_features)
        )
        partial_grad = times_weights_back(slope, own, other_weight)
        partial_grad, slope_late = lax.optimization_barrier((partial_grad, slope))
        grad_shares = lax.all_to_all(
            partial_grad.reshape(cols // 2, mine_b, -1),
            "col", 0, 0, axis_index_groups=cores,
        )

        features_all = jnp.concatenate([features, other_features])
        gathered = [
            lax.all_gather(piece, "col", axis_index_groups=[[c, c + 1] for c in range(0, cols, 2)])
            for piece in jnp.split(slope_late[:, width:], 2)
        ]
        other_slope = jnp.concatenate([lax.dynamic_index_in_dim(g, 1 - k, 0, False) for g in gathered])
        slope_all = jnp.concatenate([slope_late[:, :width], other_slope])
        weight_grad = lax.dot_general(
            features_all, slope_all, (((0,), (0,)), ((), ())), preferred_element_type=F32
        )
        grad_shares, weight_grad = lax.optimization_barrier((grad_shares, weight_grad))
        feature_grad = jnp.sum(grad_shares.astype(F32), axis=0)
        return (activation, weight_grad, feature_grad)

    return shards


def solution(mesh):
    return jax.shard_map(
        make_shards(mesh.shape["row"], mesh.shape["col"]),
        mesh=mesh,
        in_specs=(P("col", None, None), P(), P("row", "col"), P("row", "col")),
        out_specs=(P("row", "col"), P("row", "col"), P("col", "row")),
        check_vma=False,
    )
```
